32 devices in a mesh: sub: 4 (over z), blk: 8 (over y, x, core).
Axes of the slice: x: 2, y: 2, z: 4, core: 2. Of those that a mesh axis runs over, the one named last changes fastest.
Arguments:
- double_layer: bfloat16 [4, 2, 2048, 2048], P('sub', None, 'blk'), may hold values from -1 to 2
- single_layer: bfloat16 [4, 2, 2048, 2048], P('sub', None, 'blk'), may hold values from -1 to 2
- hypersingular: bfloat16 [4, 2, 2048, 2048], P('sub', None, 'blk'), may hold values from -1 to 2
- adjoint_double: bfloat16 [4, 2, 2048, 2048], P('sub', None, 'blk'), may hold values from -1 to 2
- matching: int32 [4, 1024], replicated, may hold values from 0 to 1023, each once within a row
- right_side: float32 [4, 2, 2, 2048, 64], P('sub', None, None, 'blk'), may hold values from -6 to 6
- start: float32 [4, 2, 2, 2048, 64], P('sub', None, None, 'blk'), may hold values from -4 to 4
Outputs:
- solution: float32 [4, 2, 2, 2048, 64], P('sub', None, None, 'blk')
The draws below stay inside these ranges and needn't reach their ends.
Inputs may be any that keep to these rules, and one draw needn't show every extreme that they name: `matching`: each row is a permutation of 0 to 1023; row 0 pairs with no subdomain below and is not read.
All inputs are finite; a program needn't handle non-finite values.
Results may differ from the reference program's by a relative error of at most 0.015.
Values may be sent and summed in bfloat16 or wider, within the bound.
A program may use at most 64 MiB of HBM per device.

```python
import math
import jax
import jax.numpy as jnp
from jax import lax

NH = 2048
RHS = 64
BASIS = 5
SUB = 4
HALF = 1024


def operator_block(key, salt):
    inner_key = jax.random.fold_in(key, salt)
    noise_key, diagonal_key = jax.random.split(inner_key)
    noise = jnp.clip(jax.random.normal(noise_key, (SUB, 2, NH, NH), jnp.float32), -2.0, 2.0) * (0.4 / math.sqrt(NH))
    diagonal = jax.random.uniform(diagonal_key, (SUB, NH), jnp.float32, 0.7, 1.3)
    identity = jnp.eye(NH, dtype=jnp.float32)
    real_part = noise[:, 0] + diagonal[:, :, None] * identity
    return jnp.stack([real_part, noise[:, 1]], axis=1).astype(jnp.bfloat16)


def draw_double_layer(key, part):
    return operator_block(key, 11)


def draw_single_layer(key, part):
    return operator_block(key, 23)


def draw_hypersingular(key, part):
    return operator_block(key, 37)


def draw_adjoint_double(key, part):
    return operator_block(key, 41)


def level_of(own_key, shape, cuts, least, top_value):
    def one(axis_at, blocks):
        steps = jax.random.uniform(jax.random.fold_in(jax.random.fold_in(own_key, 6), axis_at), (blocks,), jnp.float32, least / len(cuts), top_value / len(cuts))
        return jnp.repeat(jnp.exp(steps), shape[axis_at] // blocks).reshape((-1,) + (1,) * (len(shape) - axis_at - 1))

    gain = one(*cuts[0])
    for cut in cuts[1:]:
        gain = gain * one(*cut)
    return gain


def scatter_about(rng, dims, scale, reach, cuts=(), held_as=jnp.bfloat16):
    gain = level_of(rng, dims, cuts, -0.22, 0.18) if cuts else 1.0
    values = jax.random.normal(rng, dims, jnp.float32) * scale * gain
    return jnp.minimum(jnp.maximum(values, -reach), reach).astype(held_as)


def setup_inputs(seed: int = 0) -> dict:
    key_of = jax.random.split(jax.random.key(seed), 8)
    return {
        "double_layer": draw_double_layer(jax.random.fold_in(key_of[7], 71), 0),
        "single_layer": draw_single_layer(jax.random.fold_in(key_of[7], 71), 0),
        "hypersingular": draw_hypersingular(jax.random.fold_in(key_of[7], 71), 0),
        "adjoint_double": draw_adjoint_double(jax.random.fold_in(key_of[7], 71), 0),
        "matching": jax.vmap(lambda own: jax.random.permutation(own, HALF))(jax.random.split(key_of[4], SUB)).reshape((SUB, HALF)).astype(jnp.int32),
        "right_side": scatter_about(key_of[5], (SUB, 2, 2, NH, RHS), 1.0, 6.0, ((0, 4), (3, 8)), jnp.float32),
        "start": scatter_about(key_of[6], (SUB, 2, 2, NH, RHS), 0.5, 4.0, ((0, 4), (3, 8)), jnp.float32),
    }


EPSILON = 1e-06

def complex_product(matrix, vector):
    width = vector.shape[-1] // 2
    count = matrix.shape[1]
    products = jnp.dot(matrix.reshape(2 * count, matrix.shape[2]).astype(jnp.float32), vector.astype(jnp.float32), preferred_element_type=jnp.float32)
    products = products.reshape(2, count, 2 * width)
    real_part = products[0, :, :width] - products[1, :, width:]
    imag_part = products[0, :, width:] + products[1, :, :width]
    return jnp.concatenate([real_part, imag_part], axis=-1)

def calderon(double_layer, single_layer, hypersingular, adjoint_double, vector):
    upper = complex_product(single_layer, vector[1]) - complex_product(double_layer, vector[0])
    lower = complex_product(hypersingular, vector[0]) + complex_product(adjoint_double, vector[1])
    return jnp.stack([upper, lower])

def apply_all(operators, rounded):
    return lax.map(lambda pieces: calderon(*pieces), operators + (rounded,))

def take_rows(source, indices):
    return jnp.take(source, indices, axis=1)

def coupling(rounded, matching):
    odd_rows = rounded[:, :, 1::2]
    even_rows = rounded[:, :, 0::2]
    nothing = jnp.zeros_like(odd_rows[:1])
    odd_below = jnp.concatenate([nothing, odd_rows[:-1]], axis=0)
    even_above = jnp.concatenate([even_rows[1:], nothing], axis=0)
    inverse = jnp.argsort(matching, axis=1).astype(jnp.int32)
    inverse_above = jnp.concatenate([inverse[1:], inverse[:1]], axis=0)
    lower_face = jax.vmap(take_rows)(odd_below, matching)
    upper_face = jax.vmap(take_rows)(even_above, inverse_above)
    joined = jnp.stack([lower_face, upper_face], axis=3).reshape(rounded.shape).astype(jnp.float32)
    trace_signs = jnp.array([1.0, -1.0], jnp.float32).reshape(1, 2, 1, 1)
    return joined * trace_signs

def preconditioned(operators, matching, vector):
    rounded = vector.astype(jnp.bfloat16)
    middle = apply_all(operators, rounded) - 0.5 * coupling(rounded, matching)
    return apply_all(operators, middle.astype(jnp.bfloat16))

def inner(first, second):
    totals = lax.optimization_barrier(jnp.sum(first * second, axis=(0, 1, 2)))
    width = totals.shape[0] // 2
    return totals[:width] + totals[width:]

def spread(values):
    return jnp.concatenate([values, values])

def global_norm(vector):
    return jnp.sqrt(inner(vector, vector) + EPSILON)

def reference(double_layer, single_layer, hypersingular, adjoint_double, matching, right_side, start):
    operators = (double_layer, single_layer, hypersingular, adjoint_double)
    right_inner = jnp.concatenate([right_side[:, :, 0], right_side[:, :, 1]], axis=-1)
    start_inner = jnp.concatenate([start[:, :, 0], start[:, :, 1]], axis=-1)
    residual = right_inner - preconditioned(operators, matching, start_inner)
    beta = global_norm(residual)
    basis = [residual / spread(beta)]
    columns = []
    for column in range(BASIS):
        image = preconditioned(operators, matching, basis[column])
        coefficients = [inner(basis[earlier], image) for earlier in range(column + 1)]
        for earlier in range(column + 1):
            image = image - spread(coefficients[earlier]) * basis[earlier]
        height = global_norm(image)
        if column + 1 < BASIS:
            basis.append(image / spread(height))
        filler = [jnp.zeros_like(height)] * (BASIS - 1 - column)
        columns.append(jnp.stack(coefficients + [height] + filler, axis=1))
    hessen = jnp.stack(columns, axis=2)
    gram = jnp.einsum('rij,rik->rjk', hessen, hessen, precision=lax.Precision.HIGHEST)
    target = beta[:, None] * hessen[:, 0, :]
    factor = jnp.linalg.cholesky(gram)
    weights = jax.scipy.linalg.cho_solve((factor, True), target[..., None])[..., 0]
    solution = start_inner
    for column in range(BASIS):
        solution = solution + spread(weights[:, column]) * basis[column]
    width = solution.shape[-1] // 2
    return jnp.stack([solution[..., :width], solution[..., width:]], axis=2)
```

```python
import functools

import jax
import jax.numpy as jnp
from jax import lax
from jax.experimental import pallas as pl
from jax.experimental.pallas import tpu as pltpu
from jax.sharding import PartitionSpec as P

BASIS = 5
EPSILON = 1e-06
MESH = pl.DeviceIdType.MESH


def mm(a, b):
    return jnp.dot(a, b, preferred_element_type=jnp.float32)


def swap(x):
    width = x.shape[-1] // 2
    return jnp.concatenate([x[..., width:], x[..., :width]], axis=-1)


def turned(x):
    width = x.shape[-1] // 2
    return jnp.concatenate([-x[..., width:], x[..., :width]], axis=-1)


def kernel(ns, n, paired, dl, sl, hy, ad, up, down, rhs, start, out,
           buf, acc, sel, spread_sel, xs, xr, y, img, basis, coef, red1, red2,
           gsend, grecv, xsend, xrecv, r1send, r1recv, r2send, r2recv):
    s = lax.axis_index("sub")
    b = lax.axis_index("blk")
    rows = rhs.shape[3]
    total = dl.shape[3]
    half = rows // 2
    nq = n // 2 if paired else n
    chunked = rows % 128 == 0

    def blk_peer(k):
        return lax.rem(b + k, n)

    def sub_peer(k):
        return lax.rem(s + k, ns)

    def flat(ref, t):
        return jnp.concatenate([ref[0, t, 0], ref[0, t, 1]], axis=-1)

    lane = lax.broadcasted_iota(jnp.int32, (half, total), 1)
    line = lax.broadcasted_iota(jnp.int32, (half, total), 0)
    sel[pl.ds(0, half)] = jnp.where(lane == up[...], 1.0, 0.0).astype(jnp.bfloat16)
    sel[pl.ds(half, half)] = jnp.where(line == down[...], 1.0, 0.0).astype(jnp.bfloat16)
    r_at = lax.broadcasted_iota(jnp.int32, (rows, rows), 0)
    m_at = lax.broadcasted_iota(jnp.int32, (rows, rows), 1)
    goes = jnp.where(m_at < half, 2 * m_at, 2 * (m_at - half) + 1)
    spread_sel[...] = jnp.where(r_at == goes, 1.0, 0.0).astype(jnp.bfloat16)
    xr[...] = jnp.zeros_like(xr)
    basis[...] = jnp.zeros_like(basis)
    own = pl.ds(pl.multiple_of(b * rows, rows), rows)
    for t in range(2):
        buf[0, t, own, :] = flat(start, t).astype(jnp.bfloat16)

    barrier = pltpu.get_barrier_semaphore()
    for k in range(1, n):
        pl.semaphore_signal(barrier, inc=1, device_id=(s, blk_peer(k)), device_id_type=MESH)
    for k in range(1, ns):
        pl.semaphore_signal(barrier, inc=1, device_id=(sub_peer(k), b), device_id_type=MESH)
    pl.semaphore_wait(barrier, n - 1 + ns - 1)

    def block_of(owner):
        return pl.ds(pl.multiple_of(owner * rows, rows), rows)

    def send(g, owner, to, at):
        piece = buf.at[g, :, block_of(owner), :]
        return pltpu.make_async_remote_copy(
            src_ref=piece, dst_ref=piece, send_sem=gsend.at[g, at], recv_sem=grecv.at[g, at],
            device_id=(s, to), device_id_type=MESH)

    def gather(g, arrived):
        if paired:
            q, c = b // 2, lax.rem(b, 2)
            mate = 2 * q + 1 - c
            sends = [send(g, b, 2 * lax.rem(q + k, nq) + c, k) for k in range(1, nq)]
            for one in sends:
                one.start()
            mine = send(g, b, mate, nq)
            mine.start()
            sends.append(mine)
            arrived(0, b)
            mine.wait_recv()
            arrived(1, mate)
            count = 2
            for k in range(1, nq):
                sends[k - 1].wait_recv()
                far = lax.rem(q - k + nq, nq)
                on = send(g, 2 * far + c, mate, nq + k)
                on.start()
                sends.append(on)
                arrived(count, 2 * far + c)
                on.wait_recv()
                arrived(count + 1, 2 * far + 1 - c)
                count += 2
        else:
            sends = [send(g, b, blk_peer(k), k) for k in range(1, n)]
            for one in sends:
                one.start()
            arrived(0, b)
            for k in range(1, n):
                sends[k - 1].wait_recv()
                arrived(k, lax.rem(b - k + n, n))
        return sends

    def accumulate(g, where, first):
        d, m = buf[g, 0, where, :], buf[g, 1, where, :]
        for p in range(2):
            top = mm(sl[0, p, :, where], m) - mm(dl[0, p, :, where], d)
            low = mm(hy[0, p, :, where], d) + mm(ad[0, p, :, where], m)
            acc[p] = top if first else acc[p] + top
            acc[2 + p] = low if first else acc[2 + p] + low

    def pick(where, first):
        width = buf.shape[3]
        for t in range(2):
            part = mm(sel[:, where], buf[0, t, where, :])
            at = pl.ds(t * width, width)
            y[:, at] = part if first else y[:, at] + part

    everything = pl.ds(0, total)

    def couple(k_dir):
        to = s + 1 if k_dir == 0 else s - 1
        piece = pl.ds(k_dir * half, half)
        return pltpu.make_async_remote_copy(
            src_ref=xs.at[piece], dst_ref=xr.at[piece], send_sem=xsend.at[k_dir],
            recv_sem=xrecv.at[k_dir], device_id=(to, b), device_id_type=MESH)

    def step(k, carry):
        held = []

        def first_arrival(count, owner):
            where = block_of(owner)
            if chunked:
                pick(where, count == 0)
                if count < n // 2:
                    accumulate(0, where, count == 0)
                else:
                    held.append(where)

        sends = gather(0, first_arrival)
        if not chunked:
            pick(everything, True)
        xs[...] = y[...].astype(jnp.bfloat16)

        @pl.when(s < ns - 1)
        def _():
            couple(0).start()

        @pl.when(s > 0)
        def _():
            couple(1).start()

        for where in held:
            accumulate(0, where, False)
        if not chunked:
            accumulate(0, everything, True)
        for one in sends:
            one.wait_send()

        @pl.when(s < ns - 1)
        def _():
            couple(0).wait_send()
            couple(1).wait_recv()

        @pl.when(s > 0)
        def _():
            couple(1).wait_send()
            couple(0).wait_recv()

        coupled = mm(spread_sel[...], xr[...])
        width = buf.shape[3]
        for t in range(2):
            sign = -0.5 if t == 0 else 0.5
            middle = acc[2 * t] + turned(acc[2 * t + 1]) + sign * coupled[:, t * width:(t + 1) * width]
            buf[1, t, own, :] = middle.astype(jnp.bfloat16)

        def second_arrival(count, owner):
            if chunked:
                accumulate(1, block_of(owner), count == 0)

        sends = gather(1, second_arrival)
        if not chunked:
            accumulate(1, everything, True)
        for t in range(2):
            image = acc[2 * t] + turned(acc[2 * t + 1])
            img[t] = jnp.where(k == 0, flat(rhs, t) - image, image)

        par = lax.rem(k, 2)
        dots = [jnp.sum(basis[i] * img[...], axis=(0, 1))[None] for i in range(BASIS)]
        dots.append(jnp.sum(img[...] * img[...], axis=(0, 1))[None])
        dots.append(jnp.zeros((2, dots[0].shape[1]), jnp.float32))
        red1[par, b] = jnp.concatenate(dots, axis=0)
        moves = []
        for d in range(1, n):
            one = pltpu.make_async_remote_copy(
                src_ref=red1.at[par, b], dst_ref=red1.at[par, b], send_sem=r1send.at[par, d],
                recv_sem=r1recv.at[par, d], device_id=(s, blk_peer(d)), device_id_type=MESH)
            one.start()
            moves.append(one)
        for one in sends:
            one.wait_send()
        for one in moves:
            one.wait()
        red2[par, s] = jnp.sum(red1[par], axis=0)
        moves = []
        for d in range(1, ns):
            one = pltpu.make_async_remote_copy(
                src_ref=red2.at[par, s], dst_ref=red2.at[par, s], send_sem=r2send.at[par, d],
                recv_sem=r2recv.at[par, d], device_id=(sub_peer(d), b), device_id_type=MESH)
            one.start()
            moves.append(one)
        for one in moves:
            one.wait()
        summed = jnp.sum(red2[par], axis=0)
        summed = summed + swap(summed)
        squares = summed[BASIS:BASIS + 1]
        for i in range(BASIS):
            squares = squares - summed[i:i + 1] * summed[i:i + 1]
        height = jnp.sqrt(jnp.maximum(squares, 0.0) + EPSILON)
        coef[k] = jnp.concatenate([summed[:BASIS], height, jnp.zeros((2, height.shape[1]), jnp.float32)], axis=0)
        scale = 1.0 / height
        for t in range(2):
            w = img[t]
            for i in range(BASIS):
                w = w - summed[i:i + 1] * basis[i, t]
            w = w * scale
            basis[k, t] = w
            buf[0, t, own, :] = w.astype(jnp.bfloat16)
        return carry

    lax.fori_loop(0, BASIS + 1, step, 0)

    table = [coef[k] for k in range(BASIS + 1)]
    beta = table[0][BASIS:BASIS + 1]

    def entry(i, j):
        return table[j + 1][i:i + 1] if i <= j else table[j + 1][BASIS:BASIS + 1]

    low = [[None] * BASIS for _ in range(BASIS)]
    mid = []
    for j in range(BASIS):
        for l in range(j, BASIS):
            gram = sum(entry(i, j) * entry(i, l) for i in range(j + 2))
            for m in range(j):
                gram = gram - low[j][m] * low[l][m]
            if l == j:
                low[j][j] = jnp.sqrt(gram)
            else:
                low[l][j] = gram / low[j][j]
    for j in range(BASIS):
        value = beta * entry(0, j)
        for m in range(j):
            value = value - low[j][m] * mid[m]
        mid.append(value / low[j][j])
    z = [None] * BASIS
    for j in reversed(range(BASIS)):
        value = mid[j]
        for m in range(j + 1, BASIS):
            value = value - low[m][j] * z[m]
        z[j] = value / low[j][j]
    for t in range(2):
        result = flat(start, t)
        for j in range(BASIS):
            result = result + z[j] * basis[j, t]
        out[t] = result


def body(ns, n, paired, double_layer, single_layer, hypersingular, adjoint_double, matching, right_side, start):
    rows, total = double_layer.shape[2:]
    width = 2 * right_side.shape[4]
    half = rows // 2
    s = lax.axis_index("sub")
    window = lax.axis_index("blk") * half
    above = lax.dynamic_slice(matching, (jnp.minimum(s + 1, ns - 1), window), (1, half))
    up = jnp.where(s < ns - 1, 2 * above + 1, -1).reshape(half, 1)
    here = lax.dynamic_slice(matching, (s, 0), (1, matching.shape[1]))
    here = jnp.where(s > 0, here - window, -1)
    down = jnp.stack([here, jnp.full_like(here, -1)], axis=2).reshape(1, total)
    dma = pltpu.SemaphoreType.DMA
    vmem = pl.BlockSpec(memory_space=pltpu.VMEM)
    out = pl.pallas_call(
        functools.partial(kernel, ns, n, paired),
        out_shape=jax.ShapeDtypeStruct((2, rows, width), jnp.float32),
        in_specs=[vmem] * 8,
        out_specs=vmem,
        scratch_shapes=[
            pltpu.VMEM((2, 2, total, width), jnp.bfloat16),
            pltpu.VMEM((4, rows, width), jnp.float32),
            pltpu.VMEM((rows, total), jnp.bfloat16),
            pltpu.VMEM((rows, rows), jnp.bfloat16),
            pltpu.VMEM((rows, 2 * width), jnp.bfloat16),
            pltpu.VMEM((rows, 2 * width), jnp.bfloat16),
            pltpu.VMEM((rows, 2 * width), jnp.float32),
            pltpu.VMEM((2, rows, width), jnp.float32),
            pltpu.VMEM((BASIS + 1, 2, rows, width), jnp.float32),
            pltpu.VMEM((BASIS + 1, 8, width), jnp.float32),
            pltpu.VMEM((2, n, 8, width), jnp.float32),
            pltpu.VMEM((2, ns, 8, width), jnp.float32),
            dma((2, n)), dma((2, n)), dma((2,)), dma((2,)),
            dma((2, n)), dma((2, n)), dma((2, ns)), dma((2, ns)),
        ],
        compiler_params=pltpu.CompilerParams(
            collective_id=0, has_side_effects=True, vmem_limit_bytes=48 * 1024 * 1024),
    )(double_layer, single_layer, hypersingular, adjoint_double, up, down, right_side, start)
    half_width = width // 2
    return jnp.stack([out[..., :half_width], out[..., half_width:]], axis=1)[None]


def chip_pairs(mesh):
    lines = mesh.devices.reshape(mesh.shape["sub"], mesh.shape["blk"])
    if lines.shape[1] % 2:
        return False
    spots = [[tuple(getattr(d, "coords", None) or (d.id,)) for d in line] for line in lines]
    return all(line[i] == line[i + 1] for line in spots for i in range(0, len(line), 2))


def solution(mesh):
    placed = (
        P("sub", None, "blk", None),
        P("sub", None, "blk", None),
        P("sub", None, "blk", None),
        P("sub", None, "blk", None),
        P(),
        P("sub", None, None, "blk", None),
        P("sub", None, None, "blk", None),
    )
    return jax.shard_map(
        functools.partial(body, mesh.shape["sub"], mesh.shape["blk"], chip_pairs(mesh)),
        mesh=mesh,
        in_specs=placed,
        out_specs=P("sub", None, None, "blk", None),
        check_vma=False,
    )
```

```python
import functools

import jax
import jax.numpy as jnp
from jax import lax
from jax.experimental import pallas as pl
from jax.experimental.pallas import tpu as pltpu
from jax.sharding import PartitionSpec as P

BASIS = 5
EPSILON = 1e-06
MESH = pl.DeviceIdType.MESH


def mm(a, b):
    return jnp.dot(a, b, preferred_element_type=jnp.float32)


def swap(x):
    width = x.shape[-1] // 2
    return jnp.concatenate([x[..., width:], x[..., :width]], axis=-1)


def turned(x):
    width = x.shape[-1] // 2
    return jnp.concatenate([-x[..., width:], x[..., :width]], axis=-1)


def kernel(ns, n, paired, dl_in, sl_in, hy_in, ad_in, up, down, rhs, start, out,
           dl, sl, hy, ad, buf, acc, sel, spread_sel, xs, xr, y, img, basis, coef, red1, red2,
           gsend, grecv, xsend, xrecv, r1send, r1recv, r2send, r2recv, load_sem):
    s = lax.axis_index("sub")
    b = lax.axis_index("blk")
    rows = rhs.shape[3]
    total = dl_in.shape[3]
    half = rows // 2
    nq = n // 2 if paired else n
    chunked = rows % 128 == 0

    def blk_peer(k):
        return lax.rem(b + k, n)

    def sub_peer(k):
        return lax.rem(s + k, ns)

    loads = [pltpu.make_async_copy(src.at[0], dst, load_sem.at[i])
             for i, (src, dst) in enumerate(((dl_in, dl), (sl_in, sl), (hy_in, hy), (ad_in, ad)))]
    for one in loads:
        one.start()

    def flat(ref, t):
        return jnp.concatenate([ref[0, t, 0], ref[0, t, 1]], axis=-1)

    lane = lax.broadcasted_iota(jnp.int32, (half, total), 1)
    line = lax.broadcasted_iota(jnp.int32, (half, total), 0)
    sel[pl.ds(0, half)] = jnp.where(lane == up[...], 1.0, 0.0).astype(jnp.bfloat16)
    sel[pl.ds(half, half)] = jnp.where(line == down[...], 1.0, 0.0).astype(jnp.bfloat16)
    r_at = lax.broadcasted_iota(jnp.int32, (rows, rows), 0)
    m_at = lax.broadcasted_iota(jnp.int32, (rows, rows), 1)
    goes = jnp.where(m_at < half, 2 * m_at, 2 * (m_at - half) + 1)
    spread_sel[...] = jnp.where(r_at == goes, 1.0, 0.0).astype(jnp.bfloat16)
    xr[...] = jnp.zeros_like(xr)
    basis[...] = jnp.zeros_like(basis)
    own = pl.ds(pl.multiple_of(b * rows, rows), rows)
    for t in range(2):
        buf[0, t, own, :] = flat(start, t).astype(jnp.bfloat16)

    barrier = pltpu.get_barrier_semaphore()
    for k in range(1, n):
        pl.semaphore_signal(barrier, inc=1, device_id=(s, blk_peer(k)), device_id_type=MESH)
    for k in range(1, ns):
        pl.semaphore_signal(barrier, inc=1, device_id=(sub_peer(k), b), device_id_type=MESH)
    pl.semaphore_wait(barrier, n - 1 + ns - 1)

    def block_of(owner):
        return pl.ds(pl.multiple_of(owner * rows, rows), rows)

    def send(g, owner, to, at):
        piece = buf.at[g, :, block_of(owner), :]
        return pltpu.make_async_remote_copy(
            src_ref=piece, dst_ref=piece, send_sem=gsend.at[g, at], recv_sem=grecv.at[g, at],
            device_id=(s, to), device_id_type=MESH)

    def square(g, arrived, ready):
        q, c = b // 2, lax.rem(b, 2)
        along_x = 2 * (q // 2) + 1 - lax.rem(q, 2)
        along_y = lax.rem(q + 2, 4)
        near = along_x + c * (along_y - along_x)
        side = along_y + c * (along_x - along_y)
        diagonal = 3 - q
        mate = 2 * q + 1 - c

        def go(kind, piece, owner, to):
            lines = pl.ds(pl.multiple_of(owner * rows + piece % 2 * half, half), half)
            part = buf.at[g, piece // 2, lines, :]
            at = 4 * kind + piece
            one = pltpu.make_async_remote_copy(
                src_ref=part, dst_ref=part, send_sem=gsend.at[g, at], recv_sem=grecv.at[g, at],
                device_id=(s, to), device_id_type=MESH)
            sent[kind, piece] = one
            one.start()

        sent = {}
        pieces = range(4)
        for t in range(2):
            ready(t)
            for p in (2 * t, 2 * t + 1):
                go(0, p, b, 2 * near + c)
                go(1, p, b, 2 * side + c)
            for p in (2 * t, 2 * t + 1):
                go(3, p, b, mate)
        arrived(0, b)
        for p in pieces:
            sent[3, p].wait_recv()
        arrived(1, mate)
        for p in pieces:
            sent[0, p].wait_recv()
            go(2, p, 2 * near + c, 2 * side + c)
            go(4, p, 2 * near + c, mate)
        arrived(2, 2 * near + c)
        for p in pieces:
            sent[1, p].wait_recv()
            go(5, p, 2 * side + c, mate)
        arrived(3, 2 * side + c)
        for p in pieces:
            sent[2, p].wait_recv()
            go(6, p, 2 * diagonal + c, mate)
        for p in pieces:
            sent[4, p].wait_recv()
        arrived(4, 2 * side + 1 - c)
        for p in pieces:
            sent[5, p].wait_recv()
        arrived(5, 2 * near + 1 - c)
        arrived(6, 2 * diagonal + c)
        for p in pieces:
            sent[6, p].wait_recv()
        arrived(7, 2 * diagonal + 1 - c)
        return list(sent.values())

    def gather(g, arrived, ready=lambda t: None):
        if paired and n == 8:
            return square(g, arrived, ready)
        for t in range(2):
            ready(t)
        if paired:
            q, c = b // 2, lax.rem(b, 2)
            mate = 2 * q + 1 - c
            sends = [send(g, b, 2 * lax.rem(q + k, nq) + c, k) for k in range(1, nq)]
            for one in sends:
                one.start()
            mine = send(g, b, mate, nq)
            mine.start()
            sends.append(mine)
            arrived(0, b)
            mine.wait_recv()
            arrived(1, mate)
            count = 2
            for k in range(1, nq):
                sends[k - 1].wait_recv()
                far = lax.rem(q - k + nq, nq)
                on = send(g, 2 * far + c, mate, nq + k)
                on.start()
                sends.append(on)
                arrived(count, 2 * far + c)
                on.wait_recv()
                arrived(count + 1, 2 * far + 1 - c)
                count += 2
        else:
            sends = [send(g, b, blk_peer(k), k) for k in range(1, n)]
            for one in sends:
                one.start()
            arrived(0, b)
            for k in range(1, n):
                sends[k - 1].wait_recv()
                arrived(k, lax.rem(b - k + n, n))
        return sends

    def accumulate(g, where, first):
        d, m = buf[g, 0, where, :], buf[g, 1, where, :]
        for p in range(2):
            top = mm(sl[p, :, where], m) - mm(dl[p, :, where], d)
            low = mm(hy[p, :, where], d) + mm(ad[p, :, where], m)
            acc[p] = top if first else acc[p] + top
            acc[2 + p] = low if first else acc[2 + p] + low

    def pick(where, first):
        width = buf.shape[3]
        for t in range(2):
            part = mm(sel[:, where], buf[0, t, where, :])
            at = pl.ds(t * width, width)
            y[:, at] = part if first else y[:, at] + part

    everything = pl.ds(0, total)

    def couple(k_dir):
        to = s + 1 if k_dir == 0 else s - 1
        piece = pl.ds(k_dir * half, half)
        return pltpu.make_async_remote_copy(
            src_ref=xs.at[piece], dst_ref=xr.at[piece], send_sem=xsend.at[k_dir],
            recv_sem=xrecv.at[k_dir], device_id=(to, b), device_id_type=MESH)

    def step(k, carry):
        held = []

        def first_arrival(count, owner):
            where = block_of(owner)
            if count == 0:
                @pl.when(k == 0)
                def _():
                    for one in loads:
                        one.wait()
            if chunked:
                pick(where, count == 0)
                if count < n - 2:
                    accumulate(0, where, count == 0)
                else:
                    held.append(where)

        sends = gather(0, first_arrival)
        if not chunked:
            pick(everything, True)
        xs[...] = y[...].astype(jnp.bfloat16)

        @pl.when(s < ns - 1)
        def _():
            couple(0).start()

        @pl.when(s > 0)
        def _():
            couple(1).start()

        for where in held:
            accumulate(0, where, False)
        if not chunked:
            accumulate(0, everything, True)
        for one in sends:
            one.wait_send()

        @pl.when(s < ns - 1)
        def _():
            couple(0).wait_send()
            couple(1).wait_recv()

        @pl.when(s > 0)
        def _():
            couple(1).wait_send()
            couple(0).wait_recv()

        coupled = mm(spread_sel[...], xr[...])
        width = buf.shape[3]

        def store_middle(t):
            sign = -0.5 if t == 0 else 0.5
            middle = acc[2 * t] + turned(acc[2 * t + 1]) + sign * coupled[:, t * width:(t + 1) * width]
            buf[1, t, own, :] = middle.astype(jnp.bfloat16)

        def second_arrival(count, owner):
            if chunked:
                accumulate(1, block_of(owner), count == 0)

        sends = gather(1, second_arrival, store_middle)
        if not chunked:
            accumulate(1, everything, True)
        for t in range(2):
            image = acc[2 * t] + turned(acc[2 * t + 1])
            img[t] = jnp.where(k == 0, flat(rhs, t) - image, image)

        par = lax.rem(k, 2)
        dots = [jnp.sum(basis[i] * img[...], axis=(0, 1))[None] for i in range(BASIS)]
        dots.append(jnp.sum(img[...] * img[...], axis=(0, 1))[None])
        dots.append(jnp.zeros((2, dots[0].shape[1]), jnp.float32))
        red1[par, b] = jnp.concatenate(dots, axis=0)
        moves = []
        for d in range(1, n):
            one = pltpu.make_async_remote_copy(
                src_ref=red1.at[par, b], dst_ref=red1.at[par, b], send_sem=r1send.at[par, d],
                recv_sem=r1recv.at[par, d], device_id=(s, blk_peer(d)), device_id_type=MESH)
            one.start()
            moves.append(one)
        for one in sends:
            one.wait_send()
        for one in moves:
            one.wait()
        red2[par, s] = jnp.sum(red1[par], axis=0)
        moves = []
        for d in range(1, ns):
            one = pltpu.make_async_remote_copy(
                src_ref=red2.at[par, s], dst_ref=red2.at[par, s], send_sem=r2send.at[par, d],
                recv_sem=r2recv.at[par, d], device_id=(sub_peer(d), b), device_id_type=MESH)
            one.start()
            moves.append(one)
        for one in moves:
            one.wait()
        summed = jnp.sum(red2[par], axis=0)
        summed = summed + swap(summed)
        squares = summed[BASIS:BASIS + 1]
        for i in range(BASIS):
            squares = squares - summed[i:i + 1] * summed[i:i + 1]
        height = jnp.sqrt(jnp.maximum(squares, 0.0) + EPSILON)
        coef[k] = jnp.concatenate([summed[:BASIS], height, jnp.zeros((2, height.shape[1]), jnp.float32)], axis=0)
        scale = 1.0 / height
        for t in range(2):
            w = img[t]
            for i in range(BASIS):
                w = w - summed[i:i + 1] * basis[i, t]
            w = w * scale
            basis[k, t] = w
            buf[0, t, own, :] = w.astype(jnp.bfloat16)
        return carry

    lax.fori_loop(0, BASIS + 1, step, 0)

    table = [coef[k] for k in range(BASIS + 1)]
    beta = table[0][BASIS:BASIS + 1]

    def entry(i, j):
        return table[j + 1][i:i + 1] if i <= j else table[j + 1][BASIS:BASIS + 1]

    low = [[None] * BASIS for _ in range(BASIS)]
    mid = []
    for j in range(BASIS):
        for l in range(j, BASIS):
            gram = sum(entry(i, j) * entry(i, l) for i in range(j + 2))
            for m in range(j):
                gram = gram - low[j][m] * low[l][m]
            if l == j:
                low[j][j] = jnp.sqrt(gram)
            else:
                low[l][j] = gram / low[j][j]
    for j in range(BASIS):
        value = beta * entry(0, j)
        for m in range(j):
            value = value - low[j][m] * mid[m]
        mid.append(value / low[j][j])
    z = [None] * BASIS
    for j in reversed(range(BASIS)):
        value = mid[j]
        for m in range(j + 1, BASIS):
            value = value - low[m][j] * z[m]
        z[j] = value / low[j][j]
    for t in range(2):
        result = flat(start, t)
        for j in range(BASIS):
            result = result + z[j] * basis[j, t]
        out[t] = result


def body(ns, n, paired, double_layer, single_layer, hypersingular, adjoint_double, matching, right_side, start):
    rows, total = double_layer.shape[2:]
    width = 2 * right_side.shape[4]
    half = rows // 2
    s = lax.axis_index("sub")
    window = lax.axis_index("blk") * half
    above = lax.dynamic_slice(matching, (jnp.minimum(s + 1, ns - 1), window), (1, half))
    up = jnp.where(s < ns - 1, 2 * above + 1, -1).reshape(half, 1)
    here = lax.dynamic_slice(matching, (s, 0), (1, matching.shape[1]))
    here = jnp.where(s > 0, here - window, -1)
    down = jnp.stack([here, jnp.full_like(here, -1)], axis=2).reshape(1, total)
    dma = pltpu.SemaphoreType.DMA
    vmem = pl.BlockSpec(memory_space=pltpu.VMEM)
    out = pl.pallas_call(
        functools.partial(kernel, ns, n, paired),
        out_shape=jax.ShapeDtypeStruct((2, rows, width), jnp.float32),
        in_specs=[pl.BlockSpec(memory_space=pl.ANY)] * 4 + [vmem] * 4,
        out_specs=vmem,
        scratch_shapes=[pltpu.VMEM((2, rows, total), jnp.bfloat16)] * 4 + [
            pltpu.VMEM((2, 2, total, width), jnp.bfloat16),
            pltpu.VMEM((4, rows, width), jnp.float32),
            pltpu.VMEM((rows, total), jnp.bfloat16),
            pltpu.VMEM((rows, rows), jnp.bfloat16),
            pltpu.VMEM((rows, 2 * width), jnp.bfloat16),
            pltpu.VMEM((rows, 2 * width), jnp.bfloat16),
            pltpu.VMEM((rows, 2 * width), jnp.float32),
            pltpu.VMEM((2, rows, width), jnp.float32),
            pltpu.VMEM((BASIS + 1, 2, rows, width), jnp.float32),
            pltpu.VMEM((BASIS + 1, 8, width), jnp.float32),
            pltpu.VMEM((2, n, 8, width), jnp.float32),
            pltpu.VMEM((2, ns, 8, width), jnp.float32),
            dma((2, 4 * n)), dma((2, 4 * n)), dma((2,)), dma((2,)),
            dma((2, n)), dma((2, n)), dma((2, ns)), dma((2, ns)), dma((4,)),
        ],
        compiler_params=pltpu.CompilerParams(
            collective_id=0, has_side_effects=True, vmem_limit_bytes=48 * 1024 * 1024),
    )(double_layer, single_layer, hypersingular, adjoint_double, up, down, right_side, start)
    half_width = width // 2
    return jnp.stack([out[..., :half_width], out[..., half_width:]], axis=1)[None]


def chip_pairs(mesh):
    lines = mesh.devices.reshape(mesh.shape["sub"], mesh.shape["blk"])
    if lines.shape[1] % 2:
        return False
    spots = [[tuple(getattr(d, "coords", None) or (d.id,)) for d in line] for line in lines]
    return all(line[i] == line[i + 1] for line in spots for i in range(0, len(line), 2))


def solution(mesh):
    placed = (
        P("sub", None, "blk", None),
        P("sub", None, "blk", None),
        P("sub", None, "blk", None),
        P("sub", None, "blk", None),
        P(),
        P("sub", None, None, "blk", None),
        P("sub", None, None, "blk", None),
    )
    return jax.shard_map(
        functools.partial(body, mesh.shape["sub"], mesh.shape["blk"], chip_pairs(mesh)),
        mesh=mesh,
        in_specs=placed,
        out_specs=P("sub", None, None, "blk", None),
        check_vma=False,
    )
```

```python
import functools

import jax
import jax.numpy as jnp
from jax import lax
from jax.experimental import pallas as pl
from jax.experimental.pallas import tpu as pltpu
from jax.sharding import PartitionSpec as P

BASIS = 5
EPSILON = 1e-06
MESH = pl.DeviceIdType.MESH


def mm(a, b):
    return jnp.dot(a, b, preferred_element_type=jnp.float32)


def swap(x):
    width = x.shape[-1] // 2
    return jnp.concatenate([x[..., width:], x[..., :width]], axis=-1)


def turned(x):
    width = x.shape[-1] // 2
    return jnp.concatenate([-x[..., width:], x[..., :width]], axis=-1)


def kernel(ns, n, paired, dl_in, sl_in, hy_in, ad_in, up, down, rhs, start, out,
           dl, sl, hy, ad, buf, acc, sel, spread_sel, xs, xr, y, img, basis, coef, red1, red2,
           gsend, grecv, xsend, xrecv, r1send, r1recv, r2send, r2recv, load_sem):
    s = lax.axis_index("sub")
    b = lax.axis_index("blk")
    rows = rhs.shape[3]
    total = dl_in.shape[3]
    half = rows // 2
    nq = n // 2 if paired else n
    chunked = rows % 128 == 0

    def blk_peer(k):
        return lax.rem(b + k, n)

    def sub_peer(k):
        return lax.rem(s + k, ns)

    loads = [pltpu.make_async_copy(src.at[0], dst, load_sem.at[i])
             for i, (src, dst) in enumerate(((dl_in, dl), (sl_in, sl), (hy_in, hy), (ad_in, ad)))]
    for one in loads:
        one.start()

    def flat(ref, t):
        return jnp.concatenate([ref[0, t, 0], ref[0, t, 1]], axis=-1)

    lane = lax.broadcasted_iota(jnp.int32, (half, total), 1)
    line = lax.broadcasted_iota(jnp.int32, (half, total), 0)
    sel[pl.ds(0, half)] = jnp.where(lane == up[...], 1.0, 0.0).astype(jnp.bfloat16)
    sel[pl.ds(half, half)] = jnp.where(line == down[...], 1.0, 0.0).astype(jnp.bfloat16)
    r_at = lax.broadcasted_iota(jnp.int32, (rows, rows), 0)
    m_at = lax.broadcasted_iota(jnp.int32, (rows, rows), 1)
    goes = jnp.where(m_at < half, 2 * m_at, 2 * (m_at - half) + 1)
    spread_sel[...] = jnp.where(r_at == goes, 1.0, 0.0).astype(jnp.bfloat16)
    xr[...] = jnp.zeros_like(xr)
    basis[...] = jnp.zeros_like(basis)
    own = pl.ds(pl.multiple_of(b * rows, rows), rows)
    for t in range(2):
        buf[0, t, own, :] = flat(start, t).astype(jnp.bfloat16)

    barrier = pltpu.get_barrier_semaphore()
    for k in range(1, n):
        pl.semaphore_signal(barrier, inc=1, device_id=(s, blk_peer(k)), device_id_type=MESH)
    for k in range(1, ns):
        pl.semaphore_signal(barrier, inc=1, device_id=(sub_peer(k), b), device_id_type=MESH)
    pl.semaphore_wait(barrier, n - 1 + ns - 1)

    def block_of(owner):
        return pl.ds(pl.multiple_of(owner * rows, rows), rows)

    def send(g, owner, to, at):
        piece = buf.at[g, :, block_of(owner), :]
        return pltpu.make_async_remote_copy(
            src_ref=piece, dst_ref=piece, send_sem=gsend.at[g, at], recv_sem=grecv.at[g, at],
            device_id=(s, to), device_id_type=MESH)

    def square(g, arrived, ready):
        q, c = b // 2, lax.rem(b, 2)
        along_x = 2 * (q // 2) + 1 - lax.rem(q, 2)
        along_y = lax.rem(q + 2, 4)
        near = along_x + c * (along_y - along_x)
        side = along_y + c * (along_x - along_y)
        diagonal = 3 - q
        mate = 2 * q + 1 - c

        def go(kind, piece, owner, to):
            lines = pl.ds(pl.multiple_of(owner * rows + piece % 2 * half, half), half)
            part = buf.at[g, piece // 2, lines, :]
            at = 4 * kind + piece
            one = pltpu.make_async_remote_copy(
                src_ref=part, dst_ref=part, send_sem=gsend.at[g, at], recv_sem=grecv.at[g, at],
                device_id=(s, to), device_id_type=MESH)
            sent[kind, piece] = one
            one.start()

        sent = {}
        pieces = range(4)
        for t in range(2):
            ready(t)
            for p in (2 * t, 2 * t + 1):
                go(0, p, b, 2 * near + c)
                go(1, p, b, 2 * side + c)
            for p in (2 * t, 2 * t + 1):
                go(3, p, b, mate)
        arrived(0, b)
        for p in pieces:
            sent[3, p].wait_recv()
        arrived(1, mate)
        for p in pieces:
            sent[0, p].wait_recv()
            go(2, p, 2 * near + c, 2 * side + c)
            go(4, p, 2 * near + c, mate)
        arrived(2, 2 * near + c)
        for p in pieces:
            sent[1, p].wait_recv()
            go(5, p, 2 * side + c, mate)
        arrived(3, 2 * side + c)
        for p in pieces:
            sent[2, p].wait_recv()
            go(6, p, 2 * diagonal + c, mate)
        for p in pieces:
            sent[4, p].wait_recv()
        arrived(4, 2 * side + 1 - c)
        for p in pieces:
            sent[5, p].wait_recv()
        arrived(5, 2 * near + 1 - c)
        arrived(6, 2 * diagonal + c)
        for p in pieces:
            sent[6, p].wait_recv()
        arrived(7, 2 * diagonal + 1 - c)
        return list(sent.values())

    def gather(g, arrived, ready=lambda t: None):
        if paired and n == 8:
            return square(g, arrived, ready)
        for t in range(2):
            ready(t)
        if paired:
            q, c = b // 2, lax.rem(b, 2)
            mate = 2 * q + 1 - c
            sends = [send(g, b, 2 * lax.rem(q + k, nq) + c, k) for k in range(1, nq)]
            for one in sends:
                one.start()
            mine = send(g, b, mate, nq)
            mine.start()
            sends.append(mine)
            arrived(0, b)
            mine.wait_recv()
            arrived(1, mate)
            count = 2
            for k in range(1, nq):
                sends[k - 1].wait_recv()
                far = lax.rem(q - k + nq, nq)
                on = send(g, 2 * far + c, mate, nq + k)
                on.start()
                sends.append(on)
                arrived(count, 2 * far + c)
                on.wait_recv()
                arrived(count + 1, 2 * far + 1 - c)
                count += 2
        else:
            sends = [send(g, b, blk_peer(k), k) for k in range(1, n)]
            for one in sends:
                one.start()
            arrived(0, b)
            for k in range(1, n):
                sends[k - 1].wait_recv()
                arrived(k, lax.rem(b - k + n, n))
        return sends

    def accumulate(g, where, first):
        d, m = buf[g, 0, where, :], buf[g, 1, where, :]
        for p in range(2):
            top = mm(sl[p, :, where], m) - mm(dl[p, :, where], d)
            low = mm(hy[p, :, where], d) + mm(ad[p, :, where], m)
            acc[p] = top if first else acc[p] + top
            acc[2 + p] = low if first else acc[2 + p] + low

    def pick(where, first):
        width = buf.shape[3]
        for t in range(2):
            part = mm(sel[:, where], buf[0, t, where, :])
            at = pl.ds(t * width, width)
            y[:, at] = part if first else y[:, at] + part

    everything = pl.ds(0, total)

    def couple(k_dir):
        to = s + 1 if k_dir == 0 else s - 1
        piece = pl.ds(k_dir * half, half)
        return pltpu.make_async_remote_copy(
            src_ref=xs.at[piece], dst_ref=xr.at[piece], send_sem=xsend.at[k_dir],
            recv_sem=xrecv.at[k_dir], device_id=(to, b), device_id_type=MESH)

    def step(k, carry):
        held = []

        def first_arrival(count, owner):
            where = block_of(owner)
            if count == 0:
                @pl.when(k == 0)
                def _():
                    for one in loads:
                        one.wait()
            if chunked:
                pick(where, count == 0)
                if count < n - 2:
                    accumulate(0, where, count == 0)
                else:
                    held.append(where)

        def next_vector(t):
            @pl.when(k > 0)
            def _():
                past = coef[k - 1]
                w = img[t]
                for i in range(BASIS):
                    w = w - past[i:i + 1] * basis[i, t]
                w = w * (1.0 / past[BASIS:BASIS + 1])
                basis[k - 1, t] = w
                buf[0, t, own, :] = w.astype(jnp.bfloat16)

        sends = gather(0, first_arrival, next_vector)
        if not chunked:
            pick(everything, True)
        xs[...] = y[...].astype(jnp.bfloat16)

        @pl.when(s < ns - 1)
        def _():
            couple(0).start()

        @pl.when(s > 0)
        def _():
            couple(1).start()

        for where in held:
            accumulate(0, where, False)
        if not chunked:
            accumulate(0, everything, True)
        for one in sends:
            one.wait_send()

        @pl.when(s < ns - 1)
        def _():
            couple(0).wait_send()
            couple(1).wait_recv()

        @pl.when(s > 0)
        def _():
            couple(1).wait_send()
            couple(0).wait_recv()

        coupled = mm(spread_sel[...], xr[...])
        width = buf.shape[3]

        def store_middle(t):
            sign = -0.5 if t == 0 else 0.5
            middle = acc[2 * t] + turned(acc[2 * t + 1]) + sign * coupled[:, t * width:(t + 1) * width]
            buf[1, t, own, :] = middle.astype(jnp.bfloat16)

        def second_arrival(count, owner):
            if chunked:
                accumulate(1, block_of(owner), count == 0)

        sends = gather(1, second_arrival, store_middle)
        if not chunked:
            accumulate(1, everything, True)
        for t in range(2):
            image = acc[2 * t] + turned(acc[2 * t + 1])
            img[t] = jnp.where(k == 0, flat(rhs, t) - image, image)

        par = lax.rem(k, 2)
        dots = [jnp.sum(basis[i] * img[...], axis=(0, 1))[None] for i in range(BASIS)]
        dots.append(jnp.sum(img[...] * img[...], axis=(0, 1))[None])
        dots.append(jnp.zeros((2, dots[0].shape[1]), jnp.float32))
        red1[par, b] = jnp.concatenate(dots, axis=0)
        moves = []
        for d in range(1, n):
            one = pltpu.make_async_remote_copy(
                src_ref=red1.at[par, b], dst_ref=red1.at[par, b], send_sem=r1send.at[par, d],
                recv_sem=r1recv.at[par, d], device_id=(s, blk_peer(d)), device_id_type=MESH)
            one.start()
            moves.append(one)
        for one in sends:
            one.wait_send()
        for one in moves:
            one.wait()
        red2[par, s] = jnp.sum(red1[par], axis=0)
        moves = []
        for d in range(1, ns):
            one = pltpu.make_async_remote_copy(
                src_ref=red2.at[par, s], dst_ref=red2.at[par, s], send_sem=r2send.at[par, d],
                recv_sem=r2recv.at[par, d], device_id=(sub_peer(d), b), device_id_type=MESH)
            one.start()
            moves.append(one)
        for one in moves:
            one.wait()
        summed = jnp.sum(red2[par], axis=0)
        summed = summed + swap(summed)
        squares = summed[BASIS:BASIS + 1]
        for i in range(BASIS):
            squares = squares - summed[i:i + 1] * summed[i:i + 1]
        height = jnp.sqrt(jnp.maximum(squares, 0.0) + EPSILON)
        coef[k] = jnp.concatenate([summed[:BASIS], height, jnp.zeros((2, height.shape[1]), jnp.float32)], axis=0)
        return carry

    lax.fori_loop(0, BASIS + 1, step, 0)

    table = [coef[k] for k in range(BASIS + 1)]
    beta = table[0][BASIS:BASIS + 1]

    def entry(i, j):
        return table[j + 1][i:i + 1] if i <= j else table[j + 1][BASIS:BASIS + 1]

    low = [[None] * BASIS for _ in range(BASIS)]
    mid = []
    for j in range(BASIS):
        for l in range(j, BASIS):
            gram = sum(entry(i, j) * entry(i, l) for i in range(j + 2))
            for m in range(j):
                gram = gram - low[j][m] * low[l][m]
            if l == j:
                low[j][j] = jnp.sqrt(gram)
            else:
                low[l][j] = gram / low[j][j]
    for j in range(BASIS):
        value = beta * entry(0, j)
        for m in range(j):
            value = value - low[j][m] * mid[m]
        mid.append(value / low[j][j])
    z = [None] * BASIS
    for j in reversed(range(BASIS)):
        value = mid[j]
        for m in range(j + 1, BASIS):
            value = value - low[m][j] * z[m]
        z[j] = value / low[j][j]
    for t in range(2):
        result = flat(start, t)
        for j in range(BASIS):
            result = result + z[j] * basis[j, t]
        out[t] = result


def body(ns, n, paired, double_layer, single_layer, hypersingular, adjoint_double, matching, right_side, start):
    rows, total = double_layer.shape[2:]
    width = 2 * right_side.shape[4]
    half = rows // 2
    s = lax.axis_index("sub")
    window = lax.axis_index("blk") * half
    above = lax.dynamic_slice(matching, (jnp.minimum(s + 1, ns - 1), window), (1, half))
    up = jnp.where(s < ns - 1, 2 * above + 1, -1).reshape(half, 1)
    here = lax.dynamic_slice(matching, (s, 0), (1, matching.shape[1]))
    here = jnp.where(s > 0, here - window, -1)
    down = jnp.stack([here, jnp.full_like(here, -1)], axis=2).reshape(1, total)
    dma = pltpu.SemaphoreType.DMA
    vmem = pl.BlockSpec(memory_space=pltpu.VMEM)
    out = pl.pallas_call(
        functools.partial(kernel, ns, n, paired),
        out_shape=jax.ShapeDtypeStruct((2, rows, width), jnp.float32),
        in_specs=[pl.BlockSpec(memory_space=pl.ANY)] * 4 + [vmem] * 4,
        out_specs=vmem,
        scratch_shapes=[pltpu.VMEM((2, rows, total), jnp.bfloat16)] * 4 + [
            pltpu.VMEM((2, 2, total, width), jnp.bfloat16),
            pltpu.VMEM((4, rows, width), jnp.float32),
            pltpu.VMEM((rows, total), jnp.bfloat16),
            pltpu.VMEM((rows, rows), jnp.bfloat16),
            pltpu.VMEM((rows, 2 * width), jnp.bfloat16),
            pltpu.VMEM((rows, 2 * width), jnp.bfloat16),
            pltpu.VMEM((rows, 2 * width), jnp.float32),
            pltpu.VMEM((2, rows, width), jnp.float32),
            pltpu.VMEM((BASIS, 2, rows, width), jnp.float32),
            pltpu.VMEM((BASIS + 1, 8, width), jnp.float32),
            pltpu.VMEM((2, n, 8, width), jnp.float32),
            pltpu.VMEM((2, ns, 8, width), jnp.float32),
            dma((2, 4 * n)), dma((2, 4 * n)), dma((2,)), dma((2,)),
            dma((2, n)), dma((2, n)), dma((2, ns)), dma((2, ns)), dma((4,)),
        ],
        compiler_params=pltpu.CompilerParams(
            collective_id=0, has_side_effects=True, vmem_limit_bytes=48 * 1024 * 1024),
    )(double_layer, single_layer, hypersingular, adjoint_double, up, down, right_side, start)
    half_width = width // 2
    return jnp.stack([out[..., :half_width], out[..., half_width:]], axis=1)[None]


def chip_pairs(mesh):
    lines = mesh.devices.reshape(mesh.shape["sub"], mesh.shape["blk"])
    if lines.shape[1] % 2:
        return False
    spots = [[tuple(getattr(d, "coords", None) or (d.id,)) for d in line] for line in lines]
    return all(line[i] == line[i + 1] for line in spots for i in range(0, len(line), 2))


def solution(mesh):
    placed = (
        P("sub", None, "blk", None),
        P("sub", None, "blk", None),
        P("sub", None, "blk", None),
        P("sub", None, "blk", None),
        P(),
        P("sub", None, None, "blk", None),
        P("sub", None, None, "blk", None),
    )
    return jax.shard_map(
        functools.partial(body, mesh.shape["sub"], mesh.shape["blk"], chip_pairs(mesh)),
        mesh=mesh,
        in_specs=placed,
        out_specs=P("sub", None, None, "blk", None),
        check_vma=False,
    )
```
